256 devices in a mesh: outer: 32 (over z, x), inner: 8 (over y, core).
Axes of the slice: x: 4, y: 4, z: 8, core: 2. Of those that a mesh axis runs over, the one named last changes fastest.
Arguments:
- query: bfloat16 [32768, 32, 128], P(('outer', 'inner')), may hold values from -6 to 6
- keys: bfloat16 [32768, 32, 128], P(('outer', 'inner')), may hold values from -6 to 6
- value: bfloat16 [32768, 32, 128], P(('outer', 'inner')), may hold values from -6 to 6
- beta: bfloat16 [32768, 32], P(('outer', 'inner')), may hold values from 0 to 1, as said below
Outputs:
- mixed: bfloat16 [32768, 32, 128], P(('outer', 'inner'))
The draws below stay inside these ranges and needn't reach their ends.
Inputs may be any that keep to these rules, and one draw needn't show every extreme that they name: `beta`: each gate lies strictly between 0 and 1.
All inputs are finite; a program needn't handle non-finite values.
Results may differ from the reference program's by a relative error of at most 0.001.
Values may be sent and summed in bfloat16 or wider, within the bound.
No kernel may reach another device: no remote copies, remote signals or barrier semaphores. Data moves between devices by JAX's collectives and lax.ppermute only.
A program may use at most 128 MiB of HBM per device.

```python
import jax
import jax.numpy as jnp
from jax import lax

H = 32
DK = 128
SPAN = 128
SEQUENCE_TOKENS = 32768


def draw_beta(key, part):
    first, second, third, fourth, fifth_operand = jax.random.split(key, 5)
    slow_share = 0.5
    slow_head = jax.random.uniform(first, (H,)) < slow_share
    slow_rate = jax.random.uniform(second, (H,), minval=0.2, maxval=1.0) * (2.3 * DK / SEQUENCE_TOKENS)
    fast_rate = jax.random.uniform(third, (H,), minval=0.3, maxval=0.9)
    base = jnp.where(slow_head, slow_rate, fast_rate)
    factor = jnp.exp(jax.random.uniform(fourth, (SEQUENCE_TOKENS, H), minval=-0.7, maxval=0.7))
    gate_values = jnp.minimum(base[None, :] * factor, 0.98)
    token_span_block = jax.random.uniform(fifth_operand, (SEQUENCE_TOKENS, 1)) < 8.0 / SEQUENCE_TOKENS
    gate_values = jnp.where(token_span_block, 0.95, gate_values)
    return gate_values.astype(jnp.float32).astype(jnp.bfloat16)


def head_order(head_key):
    return jax.random.permutation(head_key, DK)


def draw_keys(key, part):
    values_key = jax.random.fold_in(key, 11)
    dims_key = jax.random.fold_in(key, 23)
    raw_values = jax.random.truncated_normal(values_key, -6.0, 6.0, (SEQUENCE_TOKENS, H, DK))
    ranked = jax.vmap(head_order)(jax.random.split(dims_key, H))
    weak_dims = ranked < DK // 8
    scaling = jnp.where(weak_dims, 0.05, 1.0).astype(jnp.float32)
    return (raw_values.astype(jnp.float32) * scaling[None, :, :]).astype(jnp.bfloat16)


def shard_levels(stream_key, shape, cuts, least, top_value):
    gain, own = 1.0, jax.random.fold_in(stream_key, 6)
    for axis_at, blocks in cuts:
        draws = jnp.exp(jax.random.uniform(jax.random.fold_in(own, axis_at), (blocks,), jnp.float32, least / len(cuts), top_value / len(cuts)))
        gain = gain * jnp.repeat(draws, shape[axis_at] // blocks).reshape([-1 if axis == axis_at else 1 for axis in range(len(shape))])
    return gain


def gaussian(rng, shape, spread, most, cuts=(), kind=jnp.bfloat16):
    values = spread * jax.random.normal(rng, shape, jnp.float32)
    if cuts:
        values = values * shard_levels(rng, shape, cuts, -0.22, 0.18)
    return jnp.clip(values, -most, most).astype(kind)


def setup_inputs(seed: int = 0) -> dict:
    key_of = jax.random.split(jax.random.key(seed), 5)
    query = gaussian(key_of[0], (SEQUENCE_TOKENS, H, DK), 1.0, 6.0, ((0, 256),))
    keys = draw_keys(jax.random.fold_in(key_of[4], 71), 0)
    value = gaussian(key_of[2], (SEQUENCE_TOKENS, H, DK), 1.0, 6.0, ((0, 256),))
    beta = draw_beta(jax.random.fold_in(key_of[4], 71), 0)
    return {"query": query, "keys": keys, "value": value, "beta": beta}


HIGH = lax.Precision.HIGHEST

def unit_rows(block):
    return block * lax.rsqrt(lax.optimization_barrier(jnp.sum(block * block, axis=-1, keepdims=True)) + 1e-06)

def span_terms(query_block, keys_c, value_c, beta_c):
    size = keys_c.shape[0]
    width = keys_c.shape[1]
    qnorm = unit_rows(query_block)
    knorm = unit_rows(keys_c)
    kbeta = knorm * beta_c[:, None]
    vbeta = value_c * beta_c[:, None]
    gram = jnp.dot(kbeta, knorm.T, precision=HIGH)
    lower = jnp.tril(gram, -1) + jnp.eye(size, dtype=jnp.float32)
    solved = jax.scipy.linalg.solve_triangular(lower, jnp.concatenate([kbeta, vbeta], axis=1), lower=True)
    weights = solved[:, :width]
    updates = solved[:, width:]
    scores = jnp.tril(jnp.dot(qnorm, knorm.T, precision=HIGH))
    return (qnorm, knorm, weights, updates, scores)

def reference(query, keys, value, beta):
    count = SEQUENCE_TOKENS // SPAN

    def blocks(array):
        return jnp.swapaxes(array.reshape(count, SPAN, H, DK), 1, 2)
    qblk = blocks(query)
    kblk = blocks(keys)
    vblk = blocks(value)
    bblk = jnp.swapaxes(beta.reshape(count, SPAN, H), 1, 2)
    terms_fn = jax.vmap(span_terms)

    def advance(state, inputs):
        qpart, kpart, vpart, bpart = inputs
        qnorm, knorm, weights, updates, scores = terms_fn(qpart.astype(jnp.float32), kpart.astype(jnp.float32), vpart.astype(jnp.float32), bpart.astype(jnp.float32))
        delta = updates - jnp.einsum('hcd,hde->hce', weights, state, precision=HIGH)
        result = jnp.einsum('hcd,hde->hce', qnorm, state, precision=HIGH) + jnp.einsum('hcs,hse->hce', scores, delta, precision=HIGH)
        state = state + jnp.einsum('hcd,hce->hde', knorm, delta, precision=HIGH)
        return (state, result.astype(jnp.bfloat16))
    start = jnp.zeros((H, DK, DK), jnp.float32)
    _, outputs = lax.scan(advance, start, (qblk, kblk, vblk, bblk))
    return jnp.swapaxes(outputs, 1, 2).reshape(SEQUENCE_TOKENS, H, DK)
```

```python
import functools

import jax
import jax.numpy as jnp
from jax import lax
from jax.experimental import pallas as pl
from jax.experimental.pallas import tpu as pltpu
from jax.sharding import Mesh
from jax.sharding import PartitionSpec as P

SPAN = 128
DIM = 128
SUPER = 4
STEPS = 8
PACK = 136
F32 = jnp.float32
BF16 = jnp.bfloat16
EPS = 1e-06
GROUP = ("x", "y", "core")
EVERY = ("z", "x", "y", "core")


def split(x):
    high = x.astype(BF16)
    low = (x - high.astype(F32)).astype(BF16)
    return high, low


def lanes(parts):
    return jnp.concatenate(parts, axis=1)


def rows(parts):
    return jnp.concatenate(parts, axis=0)


def mm(a, b):
    return jnp.dot(a, b, preferred_element_type=F32)


def mm_nt(a, b):
    return lax.dot_general(a, b, (((1,), (1,)), ((), ())), preferred_element_type=F32)


def mm_tn(a, b):
    return lax.dot_general(a, b, (((0,), (0,)), ((), ())), preferred_element_type=F32)


def mm_cat(a_cat, b):
    high, low = split(b)
    depth = b.shape[0]
    return mm(a_cat, rows([high, high])) + mm(a_cat[:, :depth], low)


def cat(x):
    return lanes(split(x))


def mm3(a, b):
    return mm_cat(cat(a), b)


def inv_sqrt(x):
    x = x + EPS
    guess = lax.rsqrt(x)
    return guess * (1.5 - 0.5 * x * guess * guess)


def index_grids():
    row = lax.broadcasted_iota(jnp.int32, (SPAN, SPAN), 0)
    col = lax.broadcasted_iota(jnp.int32, (SPAN, SPAN), 1)
    return row, col


def keys_kernel(kp_ref, xu_ref, w_ref, t_ref, p_ref, pcum_ref, pup_ref, carry):
    step = pl.program_id(0)
    row, col = index_grids()
    diag = row == col
    eye = jnp.where(diag, 1.0, 0.0).astype(F32)
    n = range(SUPER)

    @pl.when(step == 0)
    def _():
        for i in n:
            carry[i] = eye

    k = [kp_ref[i, 0, :SPAN, :] for i in n]
    b_row = [kp_ref[i, 0, SPAN : SPAN + 1, :].astype(F32) for i in n]
    gram = [mm_nt(k[i], k[i]) for i in n]
    on_diag = [jnp.where(diag, gram[i], 0.0) for i in n]
    r_row = [inv_sqrt(jnp.sum(on_diag[i], axis=0, keepdims=True)) for i in n]
    r_col = [inv_sqrt(jnp.sum(on_diag[i], axis=1, keepdims=True)) for i in n]
    b_col = [jnp.sum(jnp.where(diag, b_row[i], 0.0), axis=1, keepdims=True) for i in n]
    strict = [
        jnp.where(row > col, gram[i] * (b_col[i] * r_col[i]) * r_row[i], 0.0) for i in n
    ]
    x = [eye - jnp.where((row >> 1) == (col >> 1), strict[i], 0.0) for i in n]
    for level in range(1, 7):
        below = ((row >> level) ^ (col >> level)) == 1
        x_cat = [cat(x[i]) for i in n]
        part = [mm_cat(x_cat[i], jnp.where(below, strict[i], 0.0)) for i in n]
        x = [x[i] - mm3(part[i], x[i]) for i in n]
    xu = [x[i] * r_col[i] * b_row[i] for i in n]
    for i in n:
        xu_ref[i, 0] = cat(xu[i])
    w = [mm(cat(xu[i] * r_row[i]), rows([k[i], k[i]])) for i in n]
    w_split = [split(w[i]) for i in n]
    for i in n:
        w_ref[i, 0] = lanes(w_split[i])
    t = [eye - mm_tn(rows([k[i], k[i]]), rows(w_split[i])) for i in n]
    t_cat = [cat(t[i]) for i in n]
    for i in n:
        t_ref[i, 0] = t_cat[i]
    before = [carry[i] for i in n]
    for i in n:
        p_ref[i, 0] = cat(before[i])
    after = [mm_cat(t_cat[i], before[i]) for i in n]
    for i in n:
        carry[i] = after[i]

    @pl.when(step == STEPS - 1)
    def _():
        one = mm3(carry[1], carry[0])
        two = mm3(carry[3], carry[2])
        pcum_ref[0] = eye
        pcum_ref[1] = carry[0]
        pcum_ref[2] = one
        pcum_ref[3] = mm3(carry[2], one)
        pcum_ref[4] = mm3(two, one)
        pup_ref[0] = carry[1]
        pup_ref[1] = carry[2]
        pup_ref[2] = carry[3]
        pup_ref[3] = two


def values_kernel(kp_ref, v_ref, xu_ref, t_ref, pup_ref, u_ref, o_ref, ocum_ref, carry):
    step = pl.program_id(0)
    n = range(SUPER)

    @pl.when(step == 0)
    def _():
        carry[...] = jnp.zeros_like(carry)

    k = [kp_ref[i, 0, :SPAN, :] for i in n]
    v = [v_ref[i, 0] for i in n]
    u = [mm(xu_ref[i, 0], rows([v[i], v[i]])) for i in n]
    for i in n:
        u_ref[i, 0] = u[i]
    before = [carry[i] for i in n]
    for i in n:
        o_ref[i, 0] = before[i]
    own = [mm_tn(rows([k[i], k[i]]), rows(split(u[i]))) for i in n]
    for i in n:
        carry[i] = mm_cat(t_ref[i, 0], before[i]) + own[i]

    @pl.when(step == STEPS - 1)
    def _():
        one = mm3(pup_ref[0], carry[0]) + carry[1]
        two = mm3(pup_ref[2], carry[2]) + carry[3]
        ocum_ref[0] = jnp.zeros_like(one)
        ocum_ref[1] = carry[0]
        ocum_ref[2] = one
        ocum_ref[3] = mm3(pup_ref[1], one) + carry[2]
        ocum_ref[4] = mm3(pup_ref[3], one) + two


def pair_trans_kernel(up_ref, own_ref, other_ref, tup_ref, et_ref, total_ref):
    up = up_ref[0] != 0
    row, col = index_grids()
    eye = jnp.where(row == col, 1.0, 0.0).astype(F32)
    own, other = own_ref[...], other_ref[...]
    upper = jnp.where(up, own, other)
    lower = jnp.where(up, other, own)
    tup_ref[...] = upper
    et_ref[...] = jnp.where(up, other, eye)
    total_ref[...] = mm3(upper, lower)


def quad_trans_kernel(up_ref, own_ref, other_ref, et_ref, tup_ref, et_out_ref):
    up = up_ref[0] != 0
    own, other, et = own_ref[...], other_ref[...], et_ref[...]
    tup_ref[...] = jnp.where(up, own, other)
    et_out_ref[...] = jnp.where(up, mm3(et, other), et)


def pair_offset_kernel(up_ref, own_ref, other_ref, tup_ref, total_ref, eo_ref):
    up = up_ref[0] != 0
    own, other = own_ref[...], other_ref[...]
    lower = jnp.where(up, other, own)
    upper = jnp.where(up, own, other)
    total_ref[...] = mm3(tup_ref[...], lower) + upper
    eo_ref[...] = jnp.where(up, other, 0.0)


def quad_offset_kernel(up_ref, own_ref, other_ref, tup_ref, et_ref, eo_ref, total_ref, eo_out_ref):
    up = up_ref[0] != 0
    own, other, eo = own_ref[...], other_ref[...], eo_ref[...]
    lower = jnp.where(up, other, own)
    upper = jnp.where(up, own, other)
    total_ref[...] = mm3(tup_ref[...], lower) + upper
    eo_out_ref[...] = jnp.where(up, mm3(et_ref[...], other) + eo, eo)


def output_kernel(
    up_ref, other_ref, et_ref, eo_ref, pcum_ref, ocum_ref,
    q_ref, kp_ref, w_ref, u_ref, p_ref, o_ref, out_ref, start,
):
    step = pl.program_id(0)
    n = range(SUPER)

    @pl.when(step == 0)
    def _():
        eo = eo_ref[...]
        first = jnp.where(up_ref[0] != 0, mm3(et_ref[...], other_ref[...]) + eo, eo)
        for i in n:
            start[i] = mm3(pcum_ref[i], first) + ocum_ref[i]

    row, col = index_grids()
    q = [q_ref[i, 0] for i in n]
    k = [kp_ref[i, 0, :SPAN, :] for i in n]
    scale = [
        inv_sqrt(jnp.sum(jnp.square(q[i].astype(F32)), axis=1, keepdims=True)) for i in n
    ]
    scores = [split(jnp.where(row >= col, mm_nt(q[i], k[i]), 0.0)) for i in n]
    state = [mm_cat(p_ref[i, 0], start[i]) + o_ref[i, 0] for i in n]
    delta = [u_ref[i, 0] - mm_cat(w_ref[i, 0], state[i]) for i in n]
    s_split = [split(state[i]) for i in n]
    d_split = [split(delta[i]) for i in n]
    for i in n:
        left = lanes([q[i], scores[i][0]])
        total = (
            mm(left, rows([s_split[i][0], d_split[i][0]]))
            + mm(left, rows([s_split[i][1], d_split[i][1]]))
            + mm(scores[i][1], d_split[i][0])
        )
        out_ref[i, 0] = (total * scale[i]).astype(BF16)


def block(*tail):
    return pl.BlockSpec((SUPER, 1) + tail, lambda b: (0, b, 0, 0))


def whole(*shape):
    return pl.BlockSpec(shape, lambda b: (0,) * len(shape))


def like(*shape, dtype=F32):
    return jax.ShapeDtypeStruct(shape, dtype)


def cost(passes, nbytes):
    return pl.CostEstimate(
        flops=2 * SUPER * STEPS * passes * SPAN**3, bytes_accessed=nbytes, transcendentals=0
    )


SMEM = pl.BlockSpec(memory_space=pltpu.SMEM)
VMEM = pl.BlockSpec(memory_space=pltpu.VMEM)
PARAMS = pltpu.CompilerParams(vmem_limit_bytes=48 * 1024 * 1024)
MIB = 1 << 20


def small(kernel, outs, *args):
    return pl.pallas_call(
        kernel,
        out_shape=[like(DIM, DIM)] * outs,
        in_specs=[SMEM] + [VMEM] * (len(args) - 1),
        out_specs=[VMEM] * outs,
        cost_estimate=pl.CostEstimate(
            flops=12 * DIM**3, bytes_accessed=65536 * len(args), transcendentals=0
        ),
    )(*args)


def exchange(x, distance, size):
    return lax.ppermute(x, "z", [(i, i ^ distance) for i in range(size)])


def shards(query, keys, value, beta):
    depth = lax.axis_size("z")
    z = lax.axis_index("z")
    up1, up2, up4 = [((z >> s) & 1).astype(jnp.int32)[None] for s in (0, 1, 2)]

    def heads_first(array):
        return jnp.transpose(array, (1, 0, 2))

    def to_heads(array):
        return lax.all_to_all(array, GROUP, split_axis=0, concat_axis=0, tiled=True)

    def by_super(array):
        return array.reshape((SUPER, STEPS) + array.shape[1:])

    gates = jnp.pad(beta.T[:, None, :], ((0, 0), (0, PACK - SPAN - 1), (0, 0)))
    packed = jnp.concatenate([heads_first(keys), gates], axis=1)
    vt, qt = heads_first(value), heads_first(query)
    kp = to_heads(packed)
    vt, kp = lax.optimization_barrier((vt, kp))
    vh = to_heads(vt)
    qt, vh = lax.optimization_barrier((qt, vh))
    qh = to_heads(qt)
    kp, vh, qh = by_super(kp), by_super(vh), by_super(qh)

    full = (SUPER, STEPS)
    xu, w, t, p, pcum, pup = pl.pallas_call(
        keys_kernel,
        grid=(STEPS,),
        in_specs=[block(PACK, DIM)],
        out_specs=[block(SPAN, 2 * SPAN)] * 4 + [whole(5, DIM, DIM), whole(4, DIM, DIM)],
        out_shape=[like(*full, SPAN, 2 * SPAN, dtype=BF16)] * 4
        + [like(5, DIM, DIM), like(4, DIM, DIM)],
        scratch_shapes=[pltpu.VMEM((SUPER, DIM, DIM), F32)],
        compiler_params=PARAMS,
        cost_estimate=cost(44, 9 * MIB),
        name="keys_terms",
    )(kp)

    trans = pcum[4]
    tup1, et1, trans2 = small(pair_trans_kernel, 3, up1, trans, exchange(trans, 1, depth))
    tup2, et2 = small(quad_trans_kernel, 2, up2, trans2, exchange(trans2, 2, depth), et1)

    u, o, ocum = pl.pallas_call(
        values_kernel,
        grid=(STEPS,),
        in_specs=[
            block(PACK, DIM), block(SPAN, DIM), block(SPAN, 2 * SPAN), block(SPAN, 2 * SPAN),
            whole(4, DIM, DIM),
        ],
        out_specs=[block(SPAN, DIM)] * 2 + [whole(5, DIM, DIM)],
        out_shape=[like(*full, SPAN, DIM)] * 2 + [like(5, DIM, DIM)],
        scratch_shapes=[pltpu.VMEM((SUPER, DIM, DIM), F32)],
        compiler_params=PARAMS,
        cost_estimate=cost(7, 10 * MIB),
        name="values_terms",
    )(kp, vh, xu, t, pup)

    offset = ocum[4]
    off2, eo1 = small(pair_offset_kernel, 2, up1, offset, exchange(offset, 1, depth), tup1)
    off4, eo2 = small(
        quad_offset_kernel, 2, up2, off2, exchange(off2, 2, depth), tup2, et1, eo1
    )
    other = exchange(off4, 4, depth)

    out = pl.pallas_call(
        output_kernel,
        grid=(STEPS,),
        in_specs=[
            SMEM, whole(DIM, DIM), whole(DIM, DIM), whole(DIM, DIM),
            whole(5, DIM, DIM), whole(5, DIM, DIM),
            block(SPAN, DIM), block(PACK, DIM), block(SPAN, 2 * SPAN), block(SPAN, DIM),
            block(SPAN, 2 * SPAN), block(SPAN, DIM),
        ],
        out_specs=block(SPAN, DIM),
        out_shape=like(*full, SPAN, DIM, dtype=BF16),
        scratch_shapes=[pltpu.VMEM((SUPER, DIM, DIM), F32)],
        compiler_params=PARAMS,
        cost_estimate=cost(12, 11 * MIB),
        name="mix_output",
    )(up4, other, et2, eo2, pcum, ocum, qh, kp, w, u, p, o)
    back = to_heads(out.reshape(SUPER * STEPS, SPAN, DIM))
    return jnp.transpose(back, (1, 0, 2))


def solution(mesh):
    fine = Mesh(mesh.devices.reshape(8, 4, 4, 2), EVERY)
    placed = (P(EVERY, None, None), P(EVERY, None, None), P(EVERY, None, None), P(EVERY, None))
    return jax.shard_map(
        shards,
        mesh=fine,
        in_specs=placed,
        out_specs=P(EVERY, None, None),
        check_vma=False,
    )
```

```python
import functools

import jax
import jax.numpy as jnp
from jax import lax
from jax.experimental import pallas as pl
from jax.experimental.pallas import tpu as pltpu
from jax.sharding import Mesh
from jax.sharding import PartitionSpec as P

SPAN = 128
DIM = 128
SUPER = 4
STEPS = 8
EACH = 2
PACK = 136
F32 = jnp.float32
BF16 = jnp.bfloat16
EPS = 1e-06
GROUP = ("x", "y", "core")
EVERY = ("z", "x", "y", "core")


def split(x):
    high = x.astype(BF16)
    low = (x - high.astype(F32)).astype(BF16)
    return high, low


def lanes(parts):
    return jnp.concatenate(parts, axis=1)


def rows(parts):
    return jnp.concatenate(parts, axis=0)


def mm(a, b):
    return jnp.dot(a, b, preferred_element_type=F32)


def mm_nt(a, b):
    return lax.dot_general(a, b, (((1,), (1,)), ((), ())), preferred_element_type=F32)


def mm_tn(a, b):
    return lax.dot_general(a, b, (((0,), (0,)), ((), ())), preferred_element_type=F32)


def mm_cat(a_cat, b):
    high, low = split(b)
    depth, width = b.shape
    both = mm(a_cat[:, :depth], lanes([high, low]))
    return both[:, :width] + both[:, width:] + mm(a_cat[:, depth:], high)


def cat(x):
    return lanes(split(x))


def mm3(a, b):
    return mm_cat(cat(a), b)


def inv_sqrt(x):
    x = x + EPS
    guess = lax.rsqrt(x)
    return guess * (1.5 - 0.5 * x * guess * guess)


def index_grids():
    row = lax.broadcasted_iota(jnp.int32, (SPAN, SPAN), 0)
    col = lax.broadcasted_iota(jnp.int32, (SPAN, SPAN), 1)
    return row, col


def lanes_of(pair):
    return pair[:, :SPAN], pair[:, SPAN:]


def mm_wide_cat(left, right):
    depth = right[0].shape[0]
    return mm_wide((left[:, :depth], left[:, depth:]), right)


def mm_wide(left, right):
    width = right[0].shape[1]
    both = mm(left[0], lanes(right))
    return both[:, :width] + both[:, width:] + mm(left[1], right[0])


def unit_lower_inverses(strict, eye, row, col):
    n = range(len(strict))
    halves = [split(strict[i]) for i in n]
    x = [eye - jnp.where((row >> 1) == (col >> 1), strict[i], 0.0) for i in n]
    for level in range(1, 7):
        below = jnp.where(((row >> level) ^ (col >> level)) == 1, 1.0, 0.0).astype(BF16)
        corner = [(halves[i][0] * below, halves[i][1] * below) for i in n]
        x_split = [split(x[i]) for i in n]
        size = 1 << level
        if size < 8:
            part = [mm_wide(x_split[i], corner[i]) for i in n]
            x = [x[i] - mm_wide(split(part[i]), x_split[i]) for i in n]
            continue
        odd = range(size, SPAN, 2 * size)
        lower = [rows([x[i][a : a + size] for a in odd]) for i in n]
        part = [mm_wide(split(lower[i]), corner[i]) for i in n]
        lower = [lower[i] - mm_wide(split(part[i]), x_split[i]) for i in n]
        x = [
            rows([
                piece
                for m, a in enumerate(odd)
                for piece in (x[i][a - size : a], lower[i][m * size : (m + 1) * size])
            ])
            for i in n
        ]
    return x


def keys_kernel(
    kp_ref, xu_ref, yw_ref, n_ref, t_ref, p_ref, c_ref, pcum_ref, suf_ref, total_ref,
    carry, held,
):
    step = pl.program_id(0)
    row, col = index_grids()
    diag = row == col
    eye = jnp.where(diag, 1.0, 0.0).astype(F32)
    unit = eye.astype(BF16)
    each = kp_ref.shape[1]
    cells = [(i, j) for j in range(each) for i in range(SUPER)]
    n = range(len(cells))

    @pl.when(step == 0)
    def _():
        for i in range(SUPER):
            carry[i] = eye
            for j in range(each):
                held[i, j] = lanes([unit, jnp.zeros_like(unit)])

    state = [carry[i] for i in range(SUPER)]
    for c in cells:
        state[c[0]] = mm_cat(held[c], state[c[0]])
    for i in range(SUPER):
        carry[i] = state[i]

    k = [kp_ref[c][:SPAN] for c in cells]
    b_row = [kp_ref[c][SPAN : SPAN + 1].astype(F32) for c in cells]
    gram = [mm_nt(k[i], k[i]) for i in n]
    flipped = [mm_nt(unit, k[i]) for i in n]
    power = [
        jnp.sum(jnp.where(diag, gram[i], 0.0), axis=0, keepdims=True) + EPS for i in n
    ]
    c_row = [b_row[i] / power[i] for i in n]
    strict = [jnp.where(row > col, gram[i] * c_row[i], 0.0) for i in n]
    x = unit_lower_inverses(strict, eye, row, col)
    xu = [split(x[i] * jnp.sqrt(power[i])) for i in n]
    x_split = [split(x[i]) for i in n]
    yw = [mm(lanes(x_split[i]), rows([k[i], k[i]])) for i in n]
    kc = [split(flipped[i] * c_row[i]) for i in n]
    yw_split = [split(yw[i]) for i in n]
    t = [cat(eye - mm_wide(kc[i], yw_split[i])) for i in n]
    for i in n:
        c = cells[i]
        xu_ref[c] = lanes(xu[i])
        yw_ref[c] = lanes(yw_split[i])
        n_ref[c] = cat(mm_wide(kc[i], xu[i]))
        c_ref[c] = c_row[i]
        t_ref[c] = t[i]
        held[c] = t[i]
    for c in cells:
        p_ref[c] = cat(state[c[0]])
        if c[1] < each - 1:
            state[c[0]] = mm_cat(t[cells.index(c)], state[c[0]])

    @pl.when(step == pl.num_programs(0) - 1)
    def _():
        last = [mm_cat(t[n[i - SUPER]], state[i]) for i in range(SUPER)]
        one = mm3(last[1], last[0])
        two = mm3(last[3], last[2])
        pcum_ref[0] = eye
        pcum_ref[1] = last[0]
        pcum_ref[2] = one
        pcum_ref[3] = mm3(last[2], one)
        total_ref[...] = mm3(two, one)
        suf_ref[0] = mm3(two, last[1])
        suf_ref[1] = two
        suf_ref[2] = last[3]
        suf_ref[3] = eye
        suf_ref[4] = last[1]
        suf_ref[5] = last[2]


def suffix_kernel(n_ref, t_ref, suf_ref, m_ref, carry):
    step = pl.program_id(0)
    each = n_ref.shape[1]

    @pl.when(step == 0)
    def _():
        for i in range(SUPER):
            carry[i] = suf_ref[i]

    state = [carry[i] for i in range(SUPER)]
    for j in reversed(range(each)):
        for i in range(SUPER):
            after = cat(state[i])
            pair = lanes_of(after)
            m_ref[i, j] = cat(mm_wide(pair, lanes_of(n_ref[i, j])))
            state[i] = mm_wide(pair, lanes_of(t_ref[i, j]))
    for i in range(SUPER):
        carry[i] = state[i]


def offset_kernel(v_ref, m_ref, total_ref):
    each = v_ref.shape[1]
    parts = []
    for i in range(SUPER):
        for j in range(each):
            v = v_ref[i, j]
            parts.append(mm(m_ref[i, j], rows([v, v])))
    while len(parts) > 1:
        parts = [parts[m] + parts[m + 1] for m in range(0, len(parts), 2)]

    @pl.when(pl.program_id(0) == 0)
    def _():
        total_ref[...] = parts[0]

    @pl.when(pl.program_id(0) > 0)
    def _():
        total_ref[...] += parts[0]


def values_kernel(v_ref, xu_ref, n_ref, t_ref, yu_ref, o_ref, end_ref, carry):
    step = pl.program_id(0)
    count, each = v_ref.shape[:2]
    cells = [(i, j) for j in range(each) for i in range(count)]
    n = range(len(cells))

    @pl.when(step == 0)
    def _():
        carry[...] = jnp.zeros_like(carry)

    v = [v_ref[c] for c in cells]
    doubled = [rows([v[i], v[i]]) for i in n]
    own = [mm(n_ref[cells[i]], doubled[i]) for i in n]
    state = [carry[i] for i in range(count)]
    for m in n:
        c = cells[m]
        o_ref[c] = state[c[0]]
        yu_ref[c] = mm(xu_ref[c], doubled[m])
        state[c[0]] = mm_cat(t_ref[c], state[c[0]]) + own[m]
    for i in range(count):
        carry[i] = state[i]

    @pl.when(step == pl.num_programs(0) - 1)
    def _():
        for i in range(count):
            end_ref[i] = state[i]


def pair_trans_kernel(up_ref, own_ref, other_ref, tup_ref, et_ref, total_ref):
    up = up_ref[0] != 0
    row, col = index_grids()
    eye = jnp.where(row == col, 1.0, 0.0).astype(F32)
    own, other = own_ref[...], other_ref[...]
    upper = jnp.where(up, own, other)
    lower = jnp.where(up, other, own)
    tup_ref[...] = upper
    et_ref[...] = jnp.where(up, other, eye)
    total_ref[...] = mm3(upper, lower)


def quad_trans_kernel(up_ref, own_ref, other_ref, et_ref, tup_ref, et_out_ref):
    up = up_ref[0] != 0
    own, other, et = own_ref[...], other_ref[...], et_ref[...]
    tup_ref[...] = jnp.where(up, own, other)
    et_out_ref[...] = jnp.where(up, mm3(et, other), et)


def pair_offset_kernel(up_ref, own_ref, other_ref, tup_ref, total_ref, eo_ref):
    up = up_ref[0] != 0
    own, other = own_ref[...], other_ref[...]
    lower = jnp.where(up, other, own)
    upper = jnp.where(up, own, other)
    total_ref[...] = mm3(tup_ref[...], lower) + upper
    eo_ref[...] = jnp.where(up, other, 0.0)


def quad_offset_kernel(up_ref, own_ref, other_ref, tup_ref, et_ref, eo_ref, total_ref, eo_out_ref):
    up = up_ref[0] != 0
    own, other, eo = own_ref[...], other_ref[...], eo_ref[...]
    lower = jnp.where(up, other, own)
    upper = jnp.where(up, own, other)
    total_ref[...] = mm3(tup_ref[...], lower) + upper
    eo_out_ref[...] = jnp.where(up, mm3(et_ref[...], other) + eo, eo)


def scores_kernel(q_ref, kp_ref, c_ref, s_ref):
    row, col = index_grids()
    for i in range(SUPER):
        for j in range(q_ref.shape[1]):
            scores = mm_nt(q_ref[i, j], kp_ref[i, j][:SPAN]) * c_ref[i, j]
            s_ref[i, j] = cat(jnp.where(row >= col, scores, 0.0))


def output_kernel(
    up_ref, other_ref, et_ref, eo_ref, pcum_ref, suf_ref, enda_ref, endb_ref,
    q_ref, s_ref, yw_ref, p_ref, yua_ref, yub_ref, oa_ref, ob_ref, out_ref, start,
):
    step = pl.program_id(0)
    each = q_ref.shape[1]
    cells = [(i, j) for j in range(each) for i in range(SUPER)]
    n = range(len(cells))

    @pl.when(step == 0)
    def _():
        eo = eo_ref[...]
        first = jnp.where(up_ref[0] != 0, mm3(et_ref[...], other_ref[...]) + eo, eo)
        start[0] = first
        start[1] = mm3(pcum_ref[1], first) + enda_ref[0]
        middle = mm3(suf_ref[4], enda_ref[0]) + enda_ref[1]
        start[2] = mm3(pcum_ref[2], first) + middle
        start[3] = mm3(pcum_ref[3], first) + (mm3(suf_ref[5], middle) + endb_ref[0])

    def half(low_ref, high_ref, c):
        return low_ref[c] if c[0] < 2 else high_ref[c[0] - 2, c[1]]

    q = [q_ref[c] for c in cells]
    scale = [
        inv_sqrt(jnp.sum(jnp.square(q[i].astype(F32)), axis=1, keepdims=True)) for i in n
    ]
    begin = [split(start[i]) for i in range(SUPER)]
    state = [mm_wide_cat(p_ref[c], begin[c[0]]) + half(oa_ref, ob_ref, c) for c in cells]
    s_split = [split(state[i]) for i in n]
    d_split = [
        split(half(yua_ref, yub_ref, cells[i]) - mm_wide_cat(yw_ref[cells[i]], s_split[i]))
        for i in n
    ]
    for i in n:
        high, low = lanes_of(s_ref[cells[i]])
        left = lanes([q[i], high])
        both = mm(left, rows([lanes(s_split[i]), lanes(d_split[i])]))
        total = both[:, :DIM] + both[:, DIM:] + mm(low, d_split[i][0])
        out_ref[cells[i]] = (total * scale[i]).astype(BF16)


def block(*tail):
    return pl.BlockSpec((SUPER, EACH) + tail, lambda b: (0, b, 0, 0))


def whole(*shape):
    return pl.BlockSpec(shape, lambda b: (0,) * len(shape))


def like(*shape, dtype=F32):
    return jax.ShapeDtypeStruct(shape, dtype)


def cost(passes, nbytes):
    return pl.CostEstimate(
        flops=2 * SUPER * STEPS * passes * SPAN**3, bytes_accessed=nbytes, transcendentals=0
    )


SMEM = pl.BlockSpec(memory_space=pltpu.SMEM)
VMEM = pl.BlockSpec(memory_space=pltpu.VMEM)
MIB = 1 << 20
PARAMS = pltpu.CompilerParams(vmem_limit_bytes=24 * MIB)
FEW = pltpu.CompilerParams(vmem_limit_bytes=2 * MIB)


def small(kernel, outs, *args):
    return pl.pallas_call(
        kernel,
        out_shape=[like(DIM, DIM)] * outs,
        in_specs=[SMEM] + [VMEM] * (len(args) - 1),
        out_specs=[VMEM] * outs,
        compiler_params=FEW,
        cost_estimate=pl.CostEstimate(
            flops=12 * DIM**3, bytes_accessed=65536 * len(args), transcendentals=0
        ),
    )(*args)


def far(*arrays):
    return [pltpu.with_memory_space_constraint(a, pltpu.HBM) for a in arrays]


def exchange(x, distance, size):
    return lax.ppermute(x, "z", [(i, i ^ distance) for i in range(size)])


def shards(query, keys, value, beta):
    depth = lax.axis_size("z")
    z = lax.axis_index("z")
    up1, up2, up4 = [((z >> s) & 1).astype(jnp.int32)[None] for s in (0, 1, 2)]

    def heads_first(array):
        return jnp.transpose(array, (1, 0, 2))

    def to_heads(array):
        return lax.all_to_all(array, GROUP, split_axis=0, concat_axis=0, tiled=True)

    def by_super(array):
        return array.reshape((SUPER, STEPS) + array.shape[1:])

    gates = jnp.pad(beta.T[:, None, :], ((0, 0), (0, PACK - SPAN - 1), (0, 0)))
    packed = jnp.concatenate([heads_first(keys), gates], axis=1)
    mixed = jnp.concatenate([heads_first(value), heads_first(query)], axis=1)
    kp = to_heads(packed)
    mixed, kp = lax.optimization_barrier((mixed, kp))
    vq = by_super(to_heads(mixed))
    kp = by_super(kp)

    full = (SUPER, STEPS)
    half = pltpu.HBM((*full, SPAN, 2 * SPAN), BF16)
    part = pltpu.HBM((*full, SPAN, DIM), F32)
    wide = block(SPAN, 2 * SPAN)
    steps = STEPS // EACH
    xu, yw, nn, t, p, c, pcum, suf, trans = pl.pallas_call(
        keys_kernel,
        grid=(steps,),
        in_specs=[block(PACK, DIM)],
        out_specs=[wide] * 5
        + [block(1, SPAN), whole(4, DIM, DIM), whole(6, DIM, DIM), whole(DIM, DIM)],
        out_shape=[half] * 5
        + [
            pltpu.HBM((*full, 1, SPAN), F32),
            pltpu.HBM((4, DIM, DIM), F32),
            pltpu.HBM((6, DIM, DIM), F32),
            like(DIM, DIM),
        ],
        scratch_shapes=[
            pltpu.VMEM((SUPER, DIM, DIM), F32),
            pltpu.VMEM((SUPER, EACH, SPAN, 2 * SPAN), BF16),
        ],
        compiler_params=PARAMS,
        cost_estimate=cost(47, 11 * MIB),
        name="keys_terms",
    )(kp)
    long = STEPS // 2
    back_block = pl.BlockSpec((SUPER, long, SPAN, 2 * SPAN), lambda b: (0, 1 - b, 0, 0))
    m = pl.pallas_call(
        suffix_kernel,
        grid=(2,),
        in_specs=[back_block, back_block, whole(6, DIM, DIM)],
        out_specs=back_block,
        out_shape=half,
        scratch_shapes=[pltpu.VMEM((SUPER, DIM, DIM), F32)],
        compiler_params=PARAMS,
        cost_estimate=cost(6, 7 * MIB),
        name="suffix_terms",
    )(*far(nn, t, suf))

    tup1, et1, trans2 = small(pair_trans_kernel, 3, up1, trans, exchange(trans, 1, depth))
    vq, trans2, m = lax.optimization_barrier((vq, trans2, m))
    tup2, et2 = small(quad_trans_kernel, 2, up2, trans2, exchange(trans2, 2, depth), et1)

    offset = pl.pallas_call(
        offset_kernel,
        grid=(steps,),
        in_specs=[block(SPAN, DIM), wide],
        out_specs=whole(DIM, DIM),
        out_shape=like(DIM, DIM),
        compiler_params=PARAMS,
        cost_estimate=cost(2, 3 * MIB),
        name="offset_total",
    )(vq, *far(m))

    vq, offset = lax.optimization_barrier((vq, offset))
    second = pl.BlockSpec((SUPER, EACH, SPAN, DIM), lambda b: (0, b, 1, 0))
    scores = pl.pallas_call(
        scores_kernel,
        grid=(steps,),
        in_specs=[second, block(PACK, DIM), block(1, SPAN)],
        out_specs=wide,
        out_shape=half,
        compiler_params=PARAMS,
        cost_estimate=cost(1, 4 * MIB),
        name="scores",
    )(vq, kp, *far(c))
    other, scores = lax.optimization_barrier((exchange(offset, 1, depth), scores))
    off2, eo1 = small(pair_offset_kernel, 2, up1, offset, other, tup1)

    def values_half(index, vq):
        count, each = SUPER // 2, STEPS // 2
        spec = pl.BlockSpec((count, each, SPAN, 2 * SPAN), lambda b: (index, b, 0, 0))
        own = pl.BlockSpec((count, each, SPAN, DIM), lambda b: (0, b, 0, 0))
        piece = pltpu.HBM((count, STEPS, SPAN, DIM), F32)
        return pl.pallas_call(
            values_kernel,
            grid=(STEPS // each,),
            in_specs=[
                pl.BlockSpec((count, each, SPAN, DIM), lambda b: (index, b, 0, 0)),
                spec, spec, spec,
            ],
            out_specs=[own, own, whole(count, DIM, DIM)],
            out_shape=[piece, piece, pltpu.HBM((count, DIM, DIM), F32)],
            scratch_shapes=[pltpu.VMEM((count, DIM, DIM), F32)],
            compiler_params=PARAMS,
            cost_estimate=cost(3, 5 * MIB),
            name="values_terms",
        )(vq, *far(xu, nn, t))

    vq, off2 = lax.optimization_barrier((vq, off2))
    yua, oa, enda = values_half(0, vq)
    other, yua, oa, enda = lax.optimization_barrier((exchange(off2, 2, depth), yua, oa, enda))
    off4, eo2 = small(quad_offset_kernel, 2, up2, off2, other, tup2, et1, eo1)
    vq, off4 = lax.optimization_barrier((vq, off4))
    yub, ob, endb = values_half(1, vq)
    other = exchange(off4, 4, depth)

    piece = pl.BlockSpec((SUPER // 2, EACH, SPAN, DIM), lambda b: (0, b, 0, 0))
    out = pl.pallas_call(
        output_kernel,
        grid=(STEPS // EACH,),
        in_specs=[
            SMEM, whole(DIM, DIM), whole(DIM, DIM), whole(DIM, DIM),
            whole(4, DIM, DIM), whole(6, DIM, DIM), whole(2, DIM, DIM), whole(2, DIM, DIM),
            second, wide, wide, wide, piece, piece, piece, piece,
        ],
        out_specs=block(SPAN, DIM),
        out_shape=like(*full, SPAN, DIM, dtype=BF16),
        scratch_shapes=[pltpu.VMEM((SUPER, DIM, DIM), F32)],
        compiler_params=PARAMS,
        cost_estimate=cost(12, 11 * MIB),
        name="mix_output",
    )(
        up4, other, et2, eo2, *far(pcum, suf, enda, endb),
        vq, *far(scores, yw, p, yua, yub, oa, ob),
    )
    back = to_heads(out.reshape(SUPER * STEPS, SPAN, DIM))
    return jnp.transpose(back, (1, 0, 2))


def solution(mesh):
    fine = Mesh(mesh.devices.reshape(8, 4, 4, 2), EVERY)
    placed = (P(EVERY, None, None), P(EVERY, None, None), P(EVERY, None, None), P(EVERY, None))
    return jax.shard_map(
        shards,
        mesh=fine,
        in_specs=placed,
        out_specs=P(EVERY, None, None),
        check_vma=False,
    )
```

```python
import functools

import jax
import jax.numpy as jnp
from jax import lax
from jax.experimental import pallas as pl
from jax.experimental.pallas import tpu as pltpu
from jax.sharding import Mesh
from jax.sharding import PartitionSpec as P

SPAN = 128
DIM = 128
SUPER = 4
STEPS = 8
EACH = 2
LONG = 4
PACK = 136
F32 = jnp.float32
BF16 = jnp.bfloat16
EPS = 1e-06
GROUP = ("x", "y", "core")
EVERY = ("z", "x", "y", "core")


def split(x):
    high = x.astype(BF16)
    low = (x - high.astype(F32)).astype(BF16)
    return high, low


def lanes(parts):
    return jnp.concatenate(parts, axis=1)


def rows(parts):
    return jnp.concatenate(parts, axis=0)


def mm(a, b):
    return jnp.dot(a, b, preferred_element_type=F32)


def mm_nt(a, b):
    return lax.dot_general(a, b, (((1,), (1,)), ((), ())), preferred_element_type=F32)


def mm_tn(a, b):
    return lax.dot_general(a, b, (((0,), (0,)), ((), ())), preferred_element_type=F32)


def mm_cat(a_cat, b):
    high, low = split(b)
    depth, width = b.shape
    both = mm(a_cat[:, :depth], lanes([high, low]))
    return both[:, :width] + both[:, width:] + mm(a_cat[:, depth:], high)


def cat(x):
    return lanes(split(x))


def mm3(a, b):
    return mm_cat(cat(a), b)


def inv_sqrt(x):
    x = x + EPS
    guess = lax.rsqrt(x)
    return guess * (1.5 - 0.5 * x * guess * guess)


def index_grids():
    row = lax.broadcasted_iota(jnp.int32, (SPAN, SPAN), 0)
    col = lax.broadcasted_iota(jnp.int32, (SPAN, SPAN), 1)
    return row, col


def lanes_of(pair):
    return pair[:, :SPAN], pair[:, SPAN:]


def mm_wide_cat(left, right):
    depth = right[0].shape[0]
    return mm_wide((left[:, :depth], left[:, depth:]), right)


def mm_wide(left, right):
    width = right[0].shape[1]
    both = mm(left[0], lanes(right))
    return both[:, :width] + both[:, width:] + mm(left[1], right[0])


def unit_lower_inverses(strict, eye, row, col):
    n = range(len(strict))
    halves = [split(strict[i]) for i in n]
    x = [eye - jnp.where((row >> 1) == (col >> 1), strict[i], 0.0) for i in n]
    for level in range(1, 7):
        below = jnp.where(((row >> level) ^ (col >> level)) == 1, 1.0, 0.0).astype(BF16)
        corner = [(halves[i][0] * below, halves[i][1] * below) for i in n]
        x_split = [split(x[i]) for i in n]
        size = 1 << level
        if size < 8:
            part = [mm_wide(x_split[i], corner[i]) for i in n]
            x = [x[i] - mm_wide(split(part[i]), x_split[i]) for i in n]
            continue
        odd = range(size, SPAN, 2 * size)
        lower = [rows([x[i][a : a + size] for a in odd]) for i in n]
        part = [mm_wide(split(lower[i]), corner[i]) for i in n]
        lower = [lower[i] - mm_wide(split(part[i]), x_split[i]) for i in n]
        x = [
            rows([
                piece
                for m, a in enumerate(odd)
                for piece in (x[i][a - size : a], lower[i][m * size : (m + 1) * size])
            ])
            for i in n
        ]
    return x


def keys_kernel(
    kp_ref, xu_ref, yw_ref, n_ref, t_ref, p_ref, c_ref, pcum_ref, suf_ref, total_ref,
    carry, held,
):
    step = pl.program_id(0)
    row, col = index_grids()
    diag = row == col
    eye = jnp.where(diag, 1.0, 0.0).astype(F32)
    unit = eye.astype(BF16)
    each = kp_ref.shape[1]
    cells = [(i, j) for j in range(each) for i in range(SUPER)]
    n = range(len(cells))

    @pl.when(step == 0)
    def _():
        for i in range(SUPER):
            carry[i] = eye
            for j in range(each):
                held[i, j] = lanes([unit, jnp.zeros_like(unit)])

    state = [carry[i] for i in range(SUPER)]
    for c in cells:
        state[c[0]] = mm_cat(held[c], state[c[0]])
    for i in range(SUPER):
        carry[i] = state[i]

    k = [kp_ref[c][:SPAN] for c in cells]
    b_row = [kp_ref[c][SPAN : SPAN + 1].astype(F32) for c in cells]
    gram = [mm_nt(k[i], k[i]) for i in n]
    flipped = [mm_nt(unit, k[i]) for i in n]
    power = [
        jnp.sum(jnp.where(diag, gram[i], 0.0), axis=0, keepdims=True) + EPS for i in n
    ]
    c_row = [b_row[i] / power[i] for i in n]
    strict = [jnp.where(row > col, gram[i] * c_row[i], 0.0) for i in n]
    x = unit_lower_inverses(strict, eye, row, col)
    xu = [split(x[i] * jnp.sqrt(power[i])) for i in n]
    x_split = [split(x[i]) for i in n]
    yw = [mm(lanes(x_split[i]), rows([k[i], k[i]])) for i in n]
    kc = [split(flipped[i] * c_row[i]) for i in n]
    yw_split = [split(yw[i]) for i in n]
    t = [cat(eye - mm_wide(kc[i], yw_split[i])) for i in n]
    for i in n:
        c = cells[i]
        xu_ref[c] = lanes(xu[i])
        yw_ref[c] = lanes(yw_split[i])
        n_ref[c] = cat(mm_wide(kc[i], xu[i]))
        c_ref[c] = c_row[i]
        t_ref[c] = t[i]
        held[c] = t[i]
    for c in cells:
        p_ref[c] = cat(state[c[0]])
        if c[1] < each - 1:
            state[c[0]] = mm_cat(t[cells.index(c)], state[c[0]])

    @pl.when(step == pl.num_programs(0) - 1)
    def _():
        last = [mm_cat(t[n[i - SUPER]], state[i]) for i in range(SUPER)]
        one = mm3(last[1], last[0])
        two = mm3(last[3], last[2])
        pcum_ref[0] = eye
        pcum_ref[1] = last[0]
        pcum_ref[2] = one
        pcum_ref[3] = mm3(last[2], one)
        total_ref[...] = mm3(two, one)
        suf_ref[0] = mm3(two, last[1])
        suf_ref[1] = two
        suf_ref[2] = last[3]
        suf_ref[3] = eye
        suf_ref[4] = last[1]
        suf_ref[5] = last[2]


def suffix_kernel(n_ref, t_ref, suf_ref, m_ref, carry):
    step = pl.program_id(0)
    each = n_ref.shape[1]

    @pl.when(step == 0)
    def _():
        for i in range(SUPER):
            carry[i] = suf_ref[i]

    state = [carry[i] for i in range(SUPER)]
    for j in reversed(range(each)):
        for i in range(SUPER):
            after = cat(state[i])
            pair = lanes_of(after)
            m_ref[i, j] = cat(mm_wide(pair, lanes_of(n_ref[i, j])))
            state[i] = mm_wide(pair, lanes_of(t_ref[i, j]))
    for i in range(SUPER):
        carry[i] = state[i]


def offset_kernel(v_ref, m_ref, total_ref):
    each = v_ref.shape[1]
    parts = []
    for i in range(SUPER):
        for j in range(each):
            v = v_ref[i, j]
            parts.append(mm(m_ref[i, j], rows([v, v])))
    while len(parts) > 1:
        parts = [parts[m] + parts[m + 1] for m in range(0, len(parts), 2)]

    @pl.when(pl.program_id(0) == 0)
    def _():
        total_ref[...] = parts[0]

    @pl.when(pl.program_id(0) > 0)
    def _():
        total_ref[...] += parts[0]


def values_kernel(v_ref, xu_ref, n_ref, t_ref, yu_ref, o_ref, end_ref, carry):
    step = pl.program_id(0)
    count, each = v_ref.shape[:2]
    cells = [(i, j) for j in range(each) for i in range(count)]
    n = range(len(cells))

    @pl.when(step == 0)
    def _():
        carry[...] = jnp.zeros_like(carry)

    v = [v_ref[c] for c in cells]
    doubled = [rows([v[i], v[i]]) for i in n]
    own = [mm(n_ref[cells[i]], doubled[i]) for i in n]
    state = [carry[i] for i in range(count)]
    for m in n:
        c = cells[m]
        o_ref[c] = state[c[0]]
        yu_ref[c] = mm(xu_ref[c], doubled[m])
        state[c[0]] = mm_cat(t_ref[c], state[c[0]]) + own[m]
    for i in range(count):
        carry[i] = state[i]

    @pl.when(step == pl.num_programs(0) - 1)
    def _():
        for i in range(count):
            end_ref[i] = state[i]


def pair_trans_kernel(up_ref, own_ref, other_ref, tup_ref, et_ref, total_ref):
    up = up_ref[0] != 0
    row, col = index_grids()
    eye = jnp.where(row == col, 1.0, 0.0).astype(F32)
    own, other = own_ref[...], other_ref[...]
    upper = jnp.where(up, own, other)
    lower = jnp.where(up, other, own)
    tup_ref[...] = upper
    et_ref[...] = jnp.where(up, other, eye)
    total_ref[...] = mm3(upper, lower)


def quad_trans_kernel(up_ref, own_ref, other_ref, et_ref, tup_ref, et_out_ref):
    up = up_ref[0] != 0
    own, other, et = own_ref[...], other_ref[...], et_ref[...]
    tup_ref[...] = jnp.where(up, own, other)
    et_out_ref[...] = jnp.where(up, mm3(et, other), et)


def pair_offset_kernel(up_ref, own_ref, other_ref, tup_ref, total_ref, eo_ref):
    up = up_ref[0] != 0
    own, other = own_ref[...], other_ref[...]
    lower = jnp.where(up, other, own)
    upper = jnp.where(up, own, other)
    total_ref[...] = mm3(tup_ref[...], lower) + upper
    eo_ref[...] = jnp.where(up, other, 0.0)


def quad_offset_kernel(up_ref, own_ref, other_ref, tup_ref, et_ref, eo_ref, total_ref, eo_out_ref):
    up = up_ref[0] != 0
    own, other, eo = own_ref[...], other_ref[...], eo_ref[...]
    lower = jnp.where(up, other, own)
    upper = jnp.where(up, own, other)
    total_ref[...] = mm3(tup_ref[...], lower) + upper
    eo_out_ref[...] = jnp.where(up, mm3(et_ref[...], other) + eo, eo)


def scores_kernel(q_ref, kp_ref, c_ref, s_ref):
    row, col = index_grids()
    for i in range(SUPER):
        for j in range(q_ref.shape[1]):
            scores = mm_nt(q_ref[i, j], kp_ref[i, j][:SPAN]) * c_ref[i, j]
            s_ref[i, j] = cat(jnp.where(row >= col, scores, 0.0))


def output_kernel(
    up_ref, other_ref, et_ref, eo_ref, pcum_ref, suf_ref, end_ref,
    q_ref, s_ref, yw_ref, p_ref, yua_ref, yub_ref, oa_ref, ob_ref, out_ref, start,
):
    step = pl.program_id(0)
    each = q_ref.shape[1]
    cells = [(i, j) for j in range(each) for i in range(SUPER)]
    n = range(len(cells))

    @pl.when(step == 0)
    def _():
        eo = eo_ref[...]
        first = jnp.where(up_ref[0] != 0, mm3(et_ref[...], other_ref[...]) + eo, eo)
        start[0] = first
        start[1] = mm3(pcum_ref[1], first) + end_ref[0]
        middle = mm3(suf_ref[4], end_ref[0]) + end_ref[1]
        start[2] = mm3(pcum_ref[2], first) + middle
        start[3] = mm3(pcum_ref[3], first) + (mm3(suf_ref[5], middle) + end_ref[2])

    def half(low_ref, high_ref, c):
        return low_ref[c] if c[0] < SUPER - 1 else high_ref[0, c[1]]

    q = [q_ref[c] for c in cells]
    scale = [
        inv_sqrt(jnp.sum(jnp.square(q[i].astype(F32)), axis=1, keepdims=True)) for i in n
    ]
    begin = [split(start[i]) for i in range(SUPER)]
    state = [mm_wide_cat(p_ref[c], begin[c[0]]) + half(oa_ref, ob_ref, c) for c in cells]
    s_split = [split(state[i]) for i in n]
    d_split = [
        split(half(yua_ref, yub_ref, cells[i]) - mm_wide_cat(yw_ref[cells[i]], s_split[i]))
        for i in n
    ]
    for i in n:
        high, low = lanes_of(s_ref[cells[i]])
        left = lanes([q[i], high])
        both = mm(left, rows([lanes(s_split[i]), lanes(d_split[i])]))
        total = both[:, :DIM] + both[:, DIM:] + mm(low, d_split[i][0])
        out_ref[cells[i]] = (total * scale[i]).astype(BF16)


def block(*tail):
    return pl.BlockSpec((SUPER, EACH) + tail, lambda b: (0, b, 0, 0))


def whole(*shape):
    return pl.BlockSpec(shape, lambda b: (0,) * len(shape))


def like(*shape, dtype=F32):
    return jax.ShapeDtypeStruct(shape, dtype)


def cost(passes, nbytes):
    return pl.CostEstimate(
        flops=2 * SUPER * STEPS * passes * SPAN**3, bytes_accessed=nbytes, transcendentals=0
    )


SMEM = pl.BlockSpec(memory_space=pltpu.SMEM)
VMEM = pl.BlockSpec(memory_space=pltpu.VMEM)
MIB = 1 << 20
PARAMS = pltpu.CompilerParams(vmem_limit_bytes=24 * MIB)
FEW = pltpu.CompilerParams(vmem_limit_bytes=2 * MIB)


def small(kernel, outs, *args):
    return pl.pallas_call(
        kernel,
        out_shape=[like(DIM, DIM)] * outs,
        in_specs=[SMEM] + [VMEM] * (len(args) - 1),
        out_specs=[VMEM] * outs,
        compiler_params=FEW,
        cost_estimate=pl.CostEstimate(
            flops=12 * DIM**3, bytes_accessed=65536 * len(args), transcendentals=0
        ),
    )(*args)


def far(*arrays):
    return [pltpu.with_memory_space_constraint(a, pltpu.HBM) for a in arrays]


def exchange(x, distance, size):
    return lax.ppermute(x, "z", [(i, i ^ distance) for i in range(size)])


def shards(query, keys, value, beta):
    depth = lax.axis_size("z")
    z = lax.axis_index("z")
    up1, up2, up4 = [((z >> s) & 1).astype(jnp.int32)[None] for s in (0, 1, 2)]

    def heads_first(array):
        return jnp.transpose(array, (1, 0, 2))

    def to_heads(array):
        return lax.all_to_all(array, GROUP, split_axis=0, concat_axis=0, tiled=True)

    def by_super(array):
        return array.reshape((SUPER, STEPS) + array.shape[1:])

    gates = jnp.pad(beta.T[:, None, :], ((0, 0), (0, PACK - SPAN - 1), (0, 0)))
    packed = jnp.concatenate([heads_first(keys), gates], axis=1)
    mixed = jnp.concatenate([heads_first(value), heads_first(query)], axis=1)
    kp = to_heads(packed)
    mixed, kp = lax.optimization_barrier((mixed, kp))
    vq = by_super(to_heads(mixed))
    kp = by_super(kp)

    full = (SUPER, STEPS)
    half = pltpu.HBM((*full, SPAN, 2 * SPAN), BF16)
    part = pltpu.HBM((*full, SPAN, DIM), F32)
    wide = block(SPAN, 2 * SPAN)
    steps = STEPS // EACH
    xu, yw, nn, t, p, c, pcum, suf, trans = pl.pallas_call(
        keys_kernel,
        grid=(steps,),
        in_specs=[block(PACK, DIM)],
        out_specs=[wide] * 5
        + [block(1, SPAN), whole(4, DIM, DIM), whole(6, DIM, DIM), whole(DIM, DIM)],
        out_shape=[half] * 5
        + [
            pltpu.HBM((*full, 1, SPAN), F32),
            pltpu.HBM((4, DIM, DIM), F32),
            pltpu.HBM((6, DIM, DIM), F32),
            like(DIM, DIM),
        ],
        scratch_shapes=[
            pltpu.VMEM((SUPER, DIM, DIM), F32),
            pltpu.VMEM((SUPER, EACH, SPAN, 2 * SPAN), BF16),
        ],
        compiler_params=PARAMS,
        cost_estimate=cost(47, 11 * MIB),
        name="keys_terms",
    )(kp)
    long = STEPS // 2
    back_block = pl.BlockSpec((SUPER, long, SPAN, 2 * SPAN), lambda b: (0, 1 - b, 0, 0))
    m = pl.pallas_call(
        suffix_kernel,
        grid=(2,),
        in_specs=[back_block, back_block, whole(6, DIM, DIM)],
        out_specs=back_block,
        out_shape=half,
        scratch_shapes=[pltpu.VMEM((SUPER, DIM, DIM), F32)],
        compiler_params=PARAMS,
        cost_estimate=cost(6, 7 * MIB),
        name="suffix_terms",
    )(*far(nn, t, suf))

    tup1, et1, trans2 = small(pair_trans_kernel, 3, up1, trans, exchange(trans, 1, depth))
    vq, trans2, m = lax.optimization_barrier((vq, trans2, m))
    tup2, et2 = small(quad_trans_kernel, 2, up2, trans2, exchange(trans2, 2, depth), et1)

    def half_of(*shape, place=0):
        return pl.BlockSpec((SUPER, LONG) + shape, lambda b: (0, b, place, 0))

    offset = pl.pallas_call(
        offset_kernel,
        grid=(STEPS // LONG,),
        in_specs=[half_of(SPAN, DIM), half_of(SPAN, 2 * SPAN)],
        out_specs=whole(DIM, DIM),
        out_shape=like(DIM, DIM),
        compiler_params=PARAMS,
        cost_estimate=cost(2, 3 * MIB),
        name="offset_total",
    )(vq, *far(m))

    vq, offset = lax.optimization_barrier((vq, offset))
    scores = pl.pallas_call(
        scores_kernel,
        grid=(STEPS // LONG,),
        in_specs=[half_of(SPAN, DIM, place=1), half_of(PACK, DIM), half_of(1, SPAN)],
        out_specs=half_of(SPAN, 2 * SPAN),
        out_shape=half,
        compiler_params=PARAMS,
        cost_estimate=cost(1, 4 * MIB),
        name="scores",
    )(vq, kp, *far(c))
    other, scores = lax.optimization_barrier((exchange(offset, 1, depth), scores))
    off2, eo1 = small(pair_offset_kernel, 2, up1, offset, other, tup1)

    def values_part(count, place, vq, pin):
        spec = pl.BlockSpec((count, LONG, SPAN, 2 * SPAN), lambda b: (place, b, 0, 0))
        own = pl.BlockSpec((count, LONG, SPAN, DIM), lambda b: (0, b, 0, 0))
        make = pltpu.HBM if pin else jax.ShapeDtypeStruct
        piece = make((count, STEPS, SPAN, DIM), F32)
        return pl.pallas_call(
            values_kernel,
            grid=(STEPS // LONG,),
            in_specs=[
                pl.BlockSpec((count, LONG, SPAN, DIM), lambda b: (place, b, 0, 0)),
                spec, spec, spec,
            ],
            out_specs=[own, own, whole(count, DIM, DIM)],
            out_shape=[piece, piece, make((count, DIM, DIM), F32)],
            scratch_shapes=[pltpu.VMEM((count, DIM, DIM), F32)],
            compiler_params=PARAMS,
            cost_estimate=cost(count, 3 * count * MIB),
            name="values_terms",
        )(vq, *far(xu, nn, t))

    vq, off2 = lax.optimization_barrier((vq, off2))
    yub, ob, _ = values_part(1, SUPER - 1, vq, True)
    other, yub, ob = lax.optimization_barrier((exchange(off2, 2, depth), yub, ob))
    off4, eo2 = small(quad_offset_kernel, 2, up2, off2, other, tup2, et1, eo1)
    vq, off4 = lax.optimization_barrier((vq, off4))
    yua, oa, end = values_part(SUPER - 1, 0, vq, False)
    other = exchange(off4, 4, depth)

    def all_of(count, *shape, place=0):
        return pl.BlockSpec((count, STEPS) + shape, lambda b: (0, 0, place, 0))

    most, one = all_of(SUPER - 1, SPAN, DIM), all_of(1, SPAN, DIM)
    pair = all_of(SUPER, SPAN, 2 * SPAN)
    out = pl.pallas_call(
        output_kernel,
        grid=(1,),
        in_specs=[
            SMEM, whole(DIM, DIM), whole(DIM, DIM), whole(DIM, DIM),
            whole(4, DIM, DIM), whole(6, DIM, DIM), whole(3, DIM, DIM),
            all_of(SUPER, SPAN, DIM, place=1), pair, pair, pair, most, one, most, one,
        ],
        out_specs=all_of(SUPER, SPAN, DIM),
        out_shape=like(*full, SPAN, DIM, dtype=BF16),
        scratch_shapes=[pltpu.VMEM((SUPER, DIM, DIM), F32)],
        compiler_params=pltpu.CompilerParams(vmem_limit_bytes=40 * MIB),
        cost_estimate=cost(12, 11 * MIB),
        name="mix_output",
    )(
        up4, other, et2, eo2, *far(pcum, suf), end,
        vq, scores, yw, p, yua, yub, oa, ob,
    )
    back = to_heads(out.reshape(SUPER * STEPS, SPAN, DIM))
    return jnp.transpose(back, (1, 0, 2))


def solution(mesh):
    fine = Mesh(mesh.devices.reshape(8, 4, 4, 2), EVERY)
    placed = (P(EVERY, None, None), P(EVERY, None, None), P(EVERY, None, None), P(EVERY, None))
    return jax.shard_map(
        shards,
        mesh=fine,
        in_specs=placed,
        out_specs=P(EVERY, None, None),
        check_vma=False,
    )
```

```python
import functools

import jax
import jax.numpy as jnp
from jax import lax
from jax.experimental import pallas as pl
from jax.experimental.pallas import tpu as pltpu
from jax.sharding import Mesh
from jax.sharding import PartitionSpec as P

SPAN = 128
DIM = 128
SUPER = 4
STEPS = 8
EACH = 2
LONG = 4
PACK = 136
F32 = jnp.float32
BF16 = jnp.bfloat16
EPS = 1e-06
GROUP = ("x", "y", "core")
EVERY = ("z", "x", "y", "core")


def split(x):
    high = x.astype(BF16)
    low = (x - high.astype(F32)).astype(BF16)
    return high, low


def lanes(parts):
    return jnp.concatenate(parts, axis=1)


def rows(parts):
    return jnp.concatenate(parts, axis=0)


def mm(a, b):
    return jnp.dot(a, b, preferred_element_type=F32)


def mm_nt(a, b):
    return lax.dot_general(a, b, (((1,), (1,)), ((), ())), preferred_element_type=F32)


def mm_tn(a, b):
    return lax.dot_general(a, b, (((0,), (0,)), ((), ())), preferred_element_type=F32)


def mm_cat(a_cat, b):
    high, low = split(b)
    depth, width = b.shape
    both = mm(a_cat[:, :depth], lanes([high, low]))
    return both[:, :width] + both[:, width:] + mm(a_cat[:, depth:], high)


def cat(x):
    return lanes(split(x))


def mm3(a, b):
    return mm_cat(cat(a), b)


def inv_sqrt(x):
    x = x + EPS
    guess = lax.rsqrt(x)
    return guess * (1.5 - 0.5 * x * guess * guess)


def index_grids():
    row = lax.broadcasted_iota(jnp.int32, (SPAN, SPAN), 0)
    col = lax.broadcasted_iota(jnp.int32, (SPAN, SPAN), 1)
    return row, col


def lanes_of(pair):
    return pair[:, :SPAN], pair[:, SPAN:]


def mm_wide_cat(left, right):
    depth = right[0].shape[0]
    return mm_wide((left[:, :depth], left[:, depth:]), right)


def mm_wide(left, right):
    width = right[0].shape[1]
    both = mm(left[0], lanes(right))
    return both[:, :width] + both[:, width:] + mm(left[1], right[0])


def unit_lower_inverses(strict, eye, row, col):
    n = range(len(strict))
    halves = [split(strict[i]) for i in n]
    x = [eye - jnp.where((row >> 1) == (col >> 1), strict[i], 0.0) for i in n]
    for level in range(1, 7):
        below = jnp.where(((row >> level) ^ (col >> level)) == 1, 1.0, 0.0).astype(BF16)
        corner = [(halves[i][0] * below, halves[i][1] * below) for i in n]
        x_split = [split(x[i]) for i in n]
        size = 1 << level
        if size < 8:
            part = [mm_wide(x_split[i], corner[i]) for i in n]
            x = [x[i] - mm_wide(split(part[i]), x_split[i]) for i in n]
            continue
        odd = range(size, SPAN, 2 * size)
        lower = [rows([x[i][a : a + size] for a in odd]) for i in n]
        part = [mm_wide(split(lower[i]), corner[i]) for i in n]
        lower = [lower[i] - mm_wide(split(part[i]), x_split[i]) for i in n]
        x = [
            rows([
                piece
                for m, a in enumerate(odd)
                for piece in (x[i][a - size : a], lower[i][m * size : (m + 1) * size])
            ])
            for i in n
        ]
    return x


def keys_kernel(
    kp_ref, xu_ref, yw_ref, n_ref, t_ref, p_ref, c_ref, pcum_ref, suf_ref, total_ref,
    carry, held,
):
    step = pl.program_id(0)
    row, col = index_grids()
    diag = row == col
    eye = jnp.where(diag, 1.0, 0.0).astype(F32)
    unit = eye.astype(BF16)
    each = kp_ref.shape[1]
    cells = [(i, j) for j in range(each) for i in range(SUPER)]
    n = range(len(cells))

    @pl.when(step == 0)
    def _():
        for i in range(SUPER):
            carry[i] = eye
            for j in range(each):
                held[i, j] = lanes([unit, jnp.zeros_like(unit)])

    state = [carry[i] for i in range(SUPER)]
    for c in cells:
        state[c[0]] = mm_cat(held[c], state[c[0]])
    for i in range(SUPER):
        carry[i] = state[i]

    k = [kp_ref[c][:SPAN] for c in cells]
    b_row = [kp_ref[c][SPAN : SPAN + 1].astype(F32) for c in cells]
    gram = [mm_nt(k[i], k[i]) for i in n]
    flipped = [mm_nt(unit, k[i]) for i in n]
    power = [
        jnp.sum(jnp.where(diag, gram[i], 0.0), axis=0, keepdims=True) + EPS for i in n
    ]
    c_row = [b_row[i] / power[i] for i in n]
    strict = [jnp.where(row > col, gram[i] * c_row[i], 0.0) for i in n]
    x = unit_lower_inverses(strict, eye, row, col)
    xu = [split(x[i] * jnp.sqrt(power[i])) for i in n]
    x_split = [split(x[i]) for i in n]
    yw = [mm(lanes(x_split[i]), rows([k[i], k[i]])) for i in n]
    kc = [split(flipped[i] * c_row[i]) for i in n]
    yw_split = [split(yw[i]) for i in n]
    t = [cat(eye - mm_wide(kc[i], yw_split[i])) for i in n]
    for i in n:
        c = cells[i]
        xu_ref[c] = lanes(xu[i])
        yw_ref[c] = lanes(yw_split[i])
        n_ref[c] = cat(mm_wide(kc[i], xu[i]))
        c_ref[c] = c_row[i]
        t_ref[c] = t[i]
        held[c] = t[i]
    for c in cells:
        p_ref[c] = cat(state[c[0]])
        if c[1] < each - 1:
            state[c[0]] = mm_cat(t[cells.index(c)], state[c[0]])

    @pl.when(step == pl.num_programs(0) - 1)
    def _():
        last = [mm_cat(t[n[i - SUPER]], state[i]) for i in range(SUPER)]
        one = mm3(last[1], last[0])
        two = mm3(last[3], last[2])
        pcum_ref[0] = eye
        pcum_ref[1] = last[0]
        pcum_ref[2] = one
        pcum_ref[3] = mm3(last[2], one)
        total_ref[...] = mm3(two, one)
        suf_ref[0] = mm3(two, last[1])
        suf_ref[1] = two
        suf_ref[2] = last[3]
        suf_ref[3] = eye
        suf_ref[4] = last[1]
        suf_ref[5] = last[2]


def suffix_kernel(n_ref, t_ref, suf_ref, m_ref, carry):
    step = pl.program_id(0)
    each = n_ref.shape[1]

    @pl.when(step == 0)
    def _():
        for i in range(SUPER):
            carry[i] = suf_ref[i]

    state = [carry[i] for i in range(SUPER)]
    for j in reversed(range(each)):
        for i in range(SUPER):
            after = cat(state[i])
            pair = lanes_of(after)
            m_ref[i, j] = cat(mm_wide(pair, lanes_of(n_ref[i, j])))
            state[i] = mm_wide(pair, lanes_of(t_ref[i, j]))
    for i in range(SUPER):
        carry[i] = state[i]


def offset_kernel(v_ref, m_ref, total_ref):
    each = v_ref.shape[1]
    parts = []
    for i in range(SUPER):
        for j in range(each):
            v = v_ref[i, j]
            parts.append(mm(m_ref[i, j], rows([v, v])))
    while len(parts) > 1:
        parts = [parts[m] + parts[m + 1] for m in range(0, len(parts), 2)]

    @pl.when(pl.program_id(0) == 0)
    def _():
        total_ref[...] = parts[0]

    @pl.when(pl.program_id(0) > 0)
    def _():
        total_ref[...] += parts[0]


def values_kernel(v_ref, xu_ref, n_ref, t_ref, yu_ref, o_ref, end_ref, carry):
    step = pl.program_id(0)
    count, each = v_ref.shape[:2]
    cells = [(i, j) for j in range(each) for i in range(count)]
    n = range(len(cells))

    @pl.when(step == 0)
    def _():
        carry[...] = jnp.zeros_like(carry)

    v = [v_ref[c] for c in cells]
    doubled = [rows([v[i], v[i]]) for i in n]
    own = [mm(n_ref[cells[i]], doubled[i]) for i in n]
    state = [carry[i] for i in range(count)]
    for m in n:
        c = cells[m]
        o_ref[c] = state[c[0]]
        yu_ref[c] = mm(xu_ref[c], doubled[m])
        state[c[0]] = mm_cat(t_ref[c], state[c[0]]) + own[m]
    for i in range(count):
        carry[i] = state[i]

    @pl.when(step == pl.num_programs(0) - 1)
    def _():
        for i in range(count):
            end_ref[i] = state[i]


def pair_trans_kernel(up_ref, own_ref, other_ref, tup_ref, et_ref, total_ref):
    up = up_ref[0] != 0
    row, col = index_grids()
    eye = jnp.where(row == col, 1.0, 0.0).astype(F32)
    own, other = own_ref[...], other_ref[...]
    upper = jnp.where(up, own, other)
    lower = jnp.where(up, other, own)
    tup_ref[...] = upper
    et_ref[...] = jnp.where(up, other, eye)
    total_ref[...] = mm3(upper, lower)


def quad_trans_kernel(up_ref, own_ref, other_ref, et_ref, tup_ref, et_out_ref):
    up = up_ref[0] != 0
    own, other, et = own_ref[...], other_ref[...], et_ref[...]
    tup_ref[...] = jnp.where(up, own, other)
    et_out_ref[...] = jnp.where(up, mm3(et, other), et)


def pair_offset_kernel(up_ref, own_ref, other_ref, tup_ref, total_ref, eo_ref):
    up = up_ref[0] != 0
    own, other = own_ref[...], other_ref[...]
    lower = jnp.where(up, other, own)
    upper = jnp.where(up, own, other)
    total_ref[...] = mm3(tup_ref[...], lower) + upper
    eo_ref[...] = jnp.where(up, other, 0.0)


def quad_offset_kernel(up_ref, own_ref, other_ref, tup_ref, et_ref, eo_ref, total_ref, eo_out_ref):
    up = up_ref[0] != 0
    own, other, eo = own_ref[...], other_ref[...], eo_ref[...]
    lower = jnp.where(up, other, own)
    upper = jnp.where(up, own, other)
    total_ref[...] = mm3(tup_ref[...], lower) + upper
    eo_out_ref[...] = jnp.where(up, mm3(et_ref[...], other) + eo, eo)


def scores_kernel(q_ref, kp_ref, c_ref, s_ref):
    row, col = index_grids()
    for i in range(SUPER):
        for j in range(q_ref.shape[1]):
            scores = mm_nt(q_ref[i, j], kp_ref[i, j][:SPAN]) * c_ref[i, j]
            s_ref[i, j] = cat(jnp.where(row >= col, scores, 0.0))


def output_kernel(
    up_ref, other_ref, et_ref, eo_ref, pcum_ref, suf_ref, end_ref,
    q_ref, s_ref, yw_ref, p_ref, yua_ref, yub_ref, oa_ref, ob_ref, out_ref, start,
):
    step = pl.program_id(0)
    each = q_ref.shape[1]
    cells = [(i, j) for j in range(each) for i in range(SUPER)]
    n = range(len(cells))

    @pl.when(step == 0)
    def _():
        eo = eo_ref[...]
        first = jnp.where(up_ref[0] != 0, mm3(et_ref[...], other_ref[...]) + eo, eo)
        start[0] = first
        start[1] = mm3(pcum_ref[1], first) + end_ref[0]
        middle = mm3(suf_ref[4], end_ref[0]) + end_ref[1]
        start[2] = mm3(pcum_ref[2], first) + middle
        start[3] = mm3(pcum_ref[3], first) + (mm3(suf_ref[5], middle) + end_ref[2])

    def half(low_ref, high_ref, c):
        return low_ref[c] if c[0] < SUPER - 1 else high_ref[0, c[1]]

    q = [q_ref[c] for c in cells]
    scale = [
        inv_sqrt(jnp.sum(jnp.square(q[i].astype(F32)), axis=1, keepdims=True)) for i in n
    ]
    begin = [split(start[i]) for i in range(SUPER)]
    state = [mm_wide_cat(p_ref[c], begin[c[0]]) + half(oa_ref, ob_ref, c) for c in cells]
    s_split = [split(state[i]) for i in n]
    d_split = [
        split(half(yua_ref, yub_ref, cells[i]) - mm_wide_cat(yw_ref[cells[i]], s_split[i]))
        for i in n
    ]
    for i in n:
        high, low = lanes_of(s_ref[cells[i]])
        left = lanes([q[i], high])
        both = mm(left, rows([lanes(s_split[i]), lanes(d_split[i])]))
        total = both[:, :DIM] + both[:, DIM:] + mm(low, d_split[i][0])
        out_ref[cells[i]] = (total * scale[i]).astype(BF16)


def block(*tail):
    return pl.BlockSpec((SUPER, EACH) + tail, lambda b: (0, b, 0, 0))


def whole(*shape):
    return pl.BlockSpec(shape, lambda b: (0,) * len(shape))


def like(*shape, dtype=F32):
    return jax.ShapeDtypeStruct(shape, dtype)


def cost(passes, nbytes):
    return pl.CostEstimate(
        flops=2 * SUPER * STEPS * passes * SPAN**3, bytes_accessed=nbytes, transcendentals=0
    )


SMEM = pl.BlockSpec(memory_space=pltpu.SMEM)
VMEM = pl.BlockSpec(memory_space=pltpu.VMEM)
MIB = 1 << 20
PARAMS = pltpu.CompilerParams(vmem_limit_bytes=24 * MIB)
FEW = pltpu.CompilerParams(vmem_limit_bytes=2 * MIB)


def small(kernel, outs, *args):
    return pl.pallas_call(
        kernel,
        out_shape=[like(DIM, DIM)] * outs,
        in_specs=[SMEM] + [VMEM] * (len(args) - 1),
        out_specs=[VMEM] * outs,
        compiler_params=FEW,
        cost_estimate=pl.CostEstimate(
            flops=12 * DIM**3, bytes_accessed=65536 * len(args), transcendentals=0
        ),
    )(*args)


def far(*arrays):
    return [pltpu.with_memory_space_constraint(a, pltpu.HBM) for a in arrays]


def exchange(x, distance, size):
    return lax.ppermute(x, "z", [(i, i ^ distance) for i in range(size)])


def shards(query, keys, value, beta):
    depth = lax.axis_size("z")
    z = lax.axis_index("z")
    up1, up2, up4 = [((z >> s) & 1).astype(jnp.int32)[None] for s in (0, 1, 2)]

    def heads_first(array):
        return jnp.transpose(array, (1, 0, 2))

    def to_heads(array):
        return lax.all_to_all(array, GROUP, split_axis=0, concat_axis=0, tiled=True)

    def by_super(array):
        return array.reshape((SUPER, STEPS) + array.shape[1:])

    gates = jnp.broadcast_to(beta.T[:, None, :], (beta.shape[1], PACK - SPAN, beta.shape[0]))
    packed = jnp.concatenate([heads_first(keys), gates], axis=1)
    mixed = jnp.concatenate([heads_first(value), heads_first(query)], axis=1)
    kp = to_heads(packed)
    mixed, kp = lax.optimization_barrier((mixed, kp))
    vq = by_super(to_heads(mixed))
    kp = by_super(kp)

    full = (SUPER, STEPS)
    half = pltpu.HBM((*full, SPAN, 2 * SPAN), BF16)
    part = pltpu.HBM((*full, SPAN, DIM), F32)
    wide = block(SPAN, 2 * SPAN)
    steps = STEPS // EACH
    xu, yw, nn, t, p, c, pcum, suf, trans = pl.pallas_call(
        keys_kernel,
        grid=(steps,),
        in_specs=[block(PACK, DIM)],
        out_specs=[wide] * 5
        + [block(1, SPAN), whole(4, DIM, DIM), whole(6, DIM, DIM), whole(DIM, DIM)],
        out_shape=[half] * 5
        + [
            pltpu.HBM((*full, 1, SPAN), F32),
            pltpu.HBM((4, DIM, DIM), F32),
            pltpu.HBM((6, DIM, DIM), F32),
            like(DIM, DIM),
        ],
        scratch_shapes=[
            pltpu.VMEM((SUPER, DIM, DIM), F32),
            pltpu.VMEM((SUPER, EACH, SPAN, 2 * SPAN), BF16),
        ],
        compiler_params=PARAMS,
        cost_estimate=cost(47, 11 * MIB),
        name="keys_terms",
    )(kp)
    long = STEPS // 2
    back_block = pl.BlockSpec((SUPER, long, SPAN, 2 * SPAN), lambda b: (0, 1 - b, 0, 0))
    m = pl.pallas_call(
        suffix_kernel,
        grid=(2,),
        in_specs=[back_block, back_block, whole(6, DIM, DIM)],
        out_specs=back_block,
        out_shape=half,
        scratch_shapes=[pltpu.VMEM((SUPER, DIM, DIM), F32)],
        compiler_params=PARAMS,
        cost_estimate=cost(6, 7 * MIB),
        name="suffix_terms",
    )(*far(nn, t, suf))

    tup1, et1, trans2 = small(pair_trans_kernel, 3, up1, trans, exchange(trans, 1, depth))
    vq, trans2, m = lax.optimization_barrier((vq, trans2, m))
    tup2, et2 = small(quad_trans_kernel, 2, up2, trans2, exchange(trans2, 2, depth), et1)

    def half_of(*shape, place=0):
        return pl.BlockSpec((SUPER, LONG) + shape, lambda b: (0, b, place, 0))

    offset = pl.pallas_call(
        offset_kernel,
        grid=(STEPS // LONG,),
        in_specs=[half_of(SPAN, DIM), half_of(SPAN, 2 * SPAN)],
        out_specs=whole(DIM, DIM),
        out_shape=like(DIM, DIM),
        compiler_params=PARAMS,
        cost_estimate=cost(2, 3 * MIB),
        name="offset_total",
    )(vq, *far(m))

    vq, offset = lax.optimization_barrier((vq, offset))
    scores = pl.pallas_call(
        scores_kernel,
        grid=(STEPS // LONG,),
        in_specs=[half_of(SPAN, DIM, place=1), half_of(PACK, DIM), half_of(1, SPAN)],
        out_specs=half_of(SPAN, 2 * SPAN),
        out_shape=half,
        compiler_params=PARAMS,
        cost_estimate=cost(1, 4 * MIB),
        name="scores",
    )(vq, kp, *far(c))
    other, scores = lax.optimization_barrier((exchange(offset, 1, depth), scores))
    off2, eo1 = small(pair_offset_kernel, 2, up1, offset, other, tup1)

    def values_part(count, place, vq, pin):
        spec = pl.BlockSpec((count, LONG, SPAN, 2 * SPAN), lambda b: (place, b, 0, 0))
        own = pl.BlockSpec((count, LONG, SPAN, DIM), lambda b: (0, b, 0, 0))
        make = pltpu.HBM if pin else jax.ShapeDtypeStruct
        piece = make((count, STEPS, SPAN, DIM), F32)
        return pl.pallas_call(
            values_kernel,
            grid=(STEPS // LONG,),
            in_specs=[
                pl.BlockSpec((count, LONG, SPAN, DIM), lambda b: (place, b, 0, 0)),
                spec, spec, spec,
            ],
            out_specs=[own, own, whole(count, DIM, DIM)],
            out_shape=[piece, piece, make((count, DIM, DIM), F32)],
            scratch_shapes=[pltpu.VMEM((count, DIM, DIM), F32)],
            compiler_params=PARAMS,
            cost_estimate=cost(count, 3 * count * MIB),
            name="values_terms",
        )(vq, *far(xu, nn, t))

    vq, off2 = lax.optimization_barrier((vq, off2))
    yub, ob, _ = values_part(1, SUPER - 1, vq, True)
    other, yub, ob = lax.optimization_barrier((exchange(off2, 2, depth), yub, ob))
    off4, eo2 = small(quad_offset_kernel, 2, up2, off2, other, tup2, et1, eo1)
    vq, off4 = lax.optimization_barrier((vq, off4))
    yua, oa, end = values_part(SUPER - 1, 0, vq, False)
    other = exchange(off4, 7, depth)

    def all_of(count, *shape, place=0):
        return pl.BlockSpec((count, STEPS) + shape, lambda b: (0, 0, place, 0))

    most, one = all_of(SUPER - 1, SPAN, DIM), all_of(1, SPAN, DIM)
    pair = all_of(SUPER, SPAN, 2 * SPAN)
    out = pl.pallas_call(
        output_kernel,
        grid=(1,),
        in_specs=[
            SMEM, whole(DIM, DIM), whole(DIM, DIM), whole(DIM, DIM),
            whole(4, DIM, DIM), whole(6, DIM, DIM), whole(3, DIM, DIM),
            all_of(SUPER, SPAN, DIM, place=1), pair, pair, pair, most, one, most, one,
        ],
        out_specs=all_of(SUPER, SPAN, DIM),
        out_shape=like(*full, SPAN, DIM, dtype=BF16),
        scratch_shapes=[pltpu.VMEM((SUPER, DIM, DIM), F32)],
        compiler_params=pltpu.CompilerParams(vmem_limit_bytes=40 * MIB),
        cost_estimate=cost(12, 11 * MIB),
        name="mix_output",
    )(
        up4, other, et2, eo2, *far(pcum, suf), end,
        vq, scores, yw, p, yua, yub, oa, ob,
    )
    back = to_heads(out.reshape(SUPER * STEPS, SPAN, DIM))
    return jnp.transpose(back, (1, 0, 2))


def solution(mesh):
    fine = Mesh(mesh.devices.reshape(8, 4, 4, 2), EVERY)
    placed = (P(EVERY, None, None), P(EVERY, None, None), P(EVERY, None, None), P(EVERY, None))
    return jax.shard_map(
        shards,
        mesh=fine,
        in_specs=placed,
        out_specs=P(EVERY, None, None),
        check_vma=False,
    )
```
